256 devices in a mesh: chan: 2 (over x_lo), elem: 8 (over y, x_hi), beam: 16 (over z, core).
Axes of the slice: x: 4 (x_hi: 2, x_lo: 2; x = x_hi * 2 + x_lo), y: 4, z: 8, core: 2. Of those that a mesh axis runs over, the one named last changes fastest.
Arguments:
- voltages: bfloat16 [2, 128, 256, 2048], P(None, 'chan', 'beam', 'elem'), may hold values from -6 to 6
- weights: bfloat16 [2, 128, 2048, 2048], P(None, 'chan', 'elem', 'beam'), may hold values from -0.09375 to 0.09375
Outputs:
- power: float32 [128, 256, 2048], P(None, ('chan', 'elem'), 'beam')
The draws below stay inside these ranges and needn't reach their ends.
All inputs are finite; a program needn't handle non-finite values.
Results may differ from the reference program's by a relative error of at most 0.012.
Values may be sent and summed in bfloat16 or wider, within the bound.
A program may use at most 128 MiB of HBM per device.

```python
import jax
import jax.numpy as jnp
from jax import lax

C = 128
E = 2048
B = 2048
TIME = 256
N_ELEM = 8


def block_scale(key, extent, split, low, top_value):
    gain = 1.0
    for position, parts in split:
        heights = jax.random.uniform(jax.random.fold_in(jax.random.fold_in(key, 6), position), (parts,), jnp.float32, low / len(split), top_value / len(split))
        gain = gain * jnp.repeat(jnp.exp(heights), extent[position] // parts).reshape((-1,) + (1,) * (len(extent) - 1 - position))
    return gain


def scatter_about(stream_key, shape, spread, limit, cuts=(), held_as=jnp.bfloat16):
    factor_of = block_scale(stream_key, shape, cuts, -0.22, 0.18) if cuts else 1.0
    values = jax.random.normal(stream_key, shape, jnp.float32) * spread * factor_of
    return jnp.minimum(jnp.maximum(values, -limit), limit).astype(held_as)


def setup_inputs(seed: int = 0) -> dict:
    streams_of = jax.random.split(jax.random.key(seed), 3)
    return {
        "voltages": scatter_about(streams_of[0], (2, C, TIME, E), 1.0, 6.0, ((1, 2), (2, 16), (3, 8))),
        "weights": scatter_about(streams_of[1], (2, C, E, B), (2 * E) ** -0.5, 0.09375, ((1, 2), (2, 8), (3, 16))),
    }


def dft_tables(channels):
    index = jnp.arange(channels, dtype=jnp.int32)
    phase = index[:, None] * index[None, :] % channels
    angle = phase.astype(jnp.float32) * (2.0 * jnp.pi / channels)
    factor = 1.0 / jnp.sqrt(jnp.float32(channels))
    return (jnp.cos(angle) * factor, jnp.sin(angle) * factor)

def reference(voltages, weights):
    width = E // N_ELEM
    starts = jnp.arange(N_ELEM, dtype=jnp.int32) * width

    def add_block(running, start):
        volt_block = lax.dynamic_slice_in_dim(voltages, start, width, 3).astype(jnp.float32)
        weight_block = lax.dynamic_slice_in_dim(weights, start, width, 2).astype(jnp.float32)
        real_part = jnp.einsum('cte,ceb->ctb', volt_block[0], weight_block[0]) - jnp.einsum('cte,ceb->ctb', volt_block[1], weight_block[1])
        imag_part = jnp.einsum('cte,ceb->ctb', volt_block[0], weight_block[1]) + jnp.einsum('cte,ceb->ctb', volt_block[1], weight_block[0])
        rounded = jnp.stack([real_part, imag_part]).astype(jnp.bfloat16)
        rounded = lax.optimization_barrier(rounded).astype(jnp.float32)
        return (running + rounded, None)
    initial = jnp.zeros((2, C, TIME, B), jnp.float32)
    summed, unused = lax.scan(add_block, initial, starts)
    beams = lax.optimization_barrier(summed.astype(jnp.bfloat16)).astype(jnp.float32)
    cosine, sine = dft_tables(C)
    real_in = beams[0].reshape(C, TIME * B)
    imag_in = beams[1].reshape(C, TIME * B)
    highest = lax.Precision.HIGHEST
    real_out = jnp.dot(cosine, real_in, precision=highest, preferred_element_type=jnp.float32) - jnp.dot(sine, imag_in, precision=highest, preferred_element_type=jnp.float32)
    imag_out = jnp.dot(sine, real_in, precision=highest, preferred_element_type=jnp.float32) + jnp.dot(cosine, imag_in, precision=highest, preferred_element_type=jnp.float32)
    power = real_out * real_out + imag_out * imag_out
    return power.reshape(C, TIME, B)
```

```python
import functools

import jax
import jax.numpy as jnp
import numpy as np
from jax import lax
from jax.experimental import pallas as pl
from jax.experimental.pallas import tpu as pltpu
from jax.sharding import PartitionSpec as P

MESH = pl.DeviceIdType.MESH

X, Y, Z = 4, 4, 8
CHUNKS = 16


def synthesis_table(channels):
    index = np.arange(channels)
    angle = (index[:, None] * index[None, :] % channels) * (2.0 * np.pi / channels)
    cosine, sine = np.cos(angle) / np.sqrt(channels), np.sin(angle) / np.sqrt(channels)
    table = np.block([[cosine, -sine], [sine, cosine]]).astype(np.float32)
    high = table.astype(jnp.bfloat16)
    low = (table - high.astype(np.float32)).astype(jnp.bfloat16)
    return np.concatenate([high, low], axis=0)


def kernel(
    volt_hbm, weight_hbm, table_ref, power_ref,
    volt, weight, part, early, late, cross, spread,
    volt_in, weight_in, z_recv, mate_recv, early_recv, late_recv, cross_recv,
    z_send, mate_send, y_send, x_send,
):
    chan, elem, beam = lax.axis_index("chan"), lax.axis_index("elem"), lax.axis_index("beam")
    z, core = beam // 2, beam % 2
    y, x_hi = elem // 2, elem % 2
    x = x_hi * 2 + chan
    per = volt.shape[1] // CHUNKS
    times = volt.shape[3]
    channels = 2 * volt.shape[1]

    def at_z(step):
        return (chan, elem, lax.rem(z + step + Z, Z) * 2 + core)

    def at_y(step):
        return (chan, lax.rem(y + step + Y, Y) * 2 + x_hi, beam)

    def at_x(step):
        to = lax.rem(x + step, X)
        return (to % 2, y * 2 + to // 2, beam)

    mate = (chan, elem, z * 2 + (1 - core))
    others = [mate, at_z(1), at_z(-1), at_y(1), at_y(-1), at_x(1), at_x(2), at_x(3)]

    def fetch_volt(k):
        at = pl.ds(k * per, per)
        return pltpu.make_async_copy(volt_hbm.at[:, at], volt.at[:, at, beam], volt_in.at[k])

    def fetch_weight(k):
        at = pl.ds(k * per, per)
        return pltpu.make_async_copy(weight_hbm.at[:, at], weight.at[:, at], weight_in.at[k])

    def send(src, dst, send_sem, recv_sem, to):
        pltpu.make_async_remote_copy(
            src_ref=src, dst_ref=dst, send_sem=send_sem, recv_sem=recv_sem, device_id=to, device_id_type=MESH
        ).start()

    def await_bytes(like, sem):
        pltpu.make_async_copy(like, like, sem).wait()

    def piece(k, owner, half=None):
        at = pl.ds(k * per, per)
        if half is None:
            return volt.at[:, at, owner]
        return volt.at[half, at, owner]

    def owner_of(side, distance):
        step = -distance if side == 0 else distance
        return lax.rem(z + step + Z, Z) * 2 + core

    def z_hop(k, side, distance):
        owner = owner_of(side, distance)
        half = side if distance == 4 else None
        if distance:
            here = piece(k, owner, half)
            await_bytes(here, z_recv.at[side, distance - 1, k])
        if distance < 4:
            there = piece(k, owner, side if distance == 3 else None)
            send(there, there, z_send.at[side], z_recv.at[side, distance, k], at_z(1 if side == 0 else -1))
        if distance or side == 0:
            here = piece(k, owner, half)
            send(here, here, mate_send, mate_recv.at[k], mate)

    def to_y(step):
        return lax.rem(y + step + Y, Y)

    def multiply(k):
        fetch_weight(k).wait()
        await_bytes(volt.at[:, pl.ds(k * per, per), pl.ds(0, 8)], mate_recv.at[k])

        @pl.loop(0, per)
        def _(c):
            at = k * per + c
            rows = volt.shape[2] * times
            width = volt.shape[4]
            volt_real = volt[0, at].reshape(rows, width)
            volt_imag = volt[1, at].reshape(rows, width)
            both = jnp.concatenate([weight[0, at], weight[1, at]], axis=1)
            beams = weight.shape[3]
            with_real = jnp.dot(volt_real, both, preferred_element_type=jnp.float32)
            with_imag = jnp.dot(volt_imag, both, preferred_element_type=jnp.float32)
            real = with_real[:, :beams] - with_imag[:, beams:]
            imag = with_real[:, beams:] + with_imag[:, :beams]
            shape = part.shape[3:]
            part[k, 0, c] = real.astype(jnp.bfloat16).reshape(shape)
            part[k, 1, c] = imag.astype(jnp.bfloat16).reshape(shape)

    def send_early(k):
        far = to_y(2)
        for side in (0, 1):
            send(
                part.at[k, side, :, :, far], early.at[k, side], y_send.at[side], early_recv.at[side, k],
                at_y(1 if side == 0 else -1),
            )

    def send_late(k):
        for side in (0, 1):
            near = to_y(1 if side == 0 else -1)
            await_bytes(early.at[k, side], early_recv.at[side, k])
            for c in range(per):
                total = part[k, side, c, :, near].astype(jnp.float32) + early[k, side, c].astype(jnp.float32)
                part[k, side, c, :, near] = total.astype(jnp.bfloat16)
            send(
                part.at[k, :, :, :, near], late.at[k, side], y_send.at[side], late_recv.at[side, k],
                at_y(1 if side == 0 else -1),
            )

    def send_cross(k):
        for side in (0, 1):
            await_bytes(late.at[k, side], late_recv.at[side, k])
        for ri in (0, 1):
            for c in range(per):
                total = (
                    part[k, ri, c, :, y].astype(jnp.float32)
                    + late[k, 0, ri, c].astype(jnp.float32)
                    + late[k, 1, ri, c].astype(jnp.float32)
                )
                part[k, ri, c, :, y] = total.astype(jnp.bfloat16)
        for step in (2, 1, 3):
            to = lax.rem(x + step, X)
            send(
                part.at[k, :, :, to % 2, y, to // 2], cross.at[k, step - 1], x_send, cross_recv.at[k], at_x(step)
            )

    def gather(k):
        await_bytes(cross.at[k], cross_recv.at[k])
        for ri in (0, 1):
            for c in range(per):
                at = k * per + c
                mine = part[k, ri, c, chan, y, x_hi].astype(jnp.float32) + cross[k, 1, ri, c].astype(jnp.float32)
                theirs = cross[k, 0, ri, c].astype(jnp.float32) + cross[k, 2, ri, c].astype(jnp.float32)
                half = channels // 2
                spread[pl.ds(ri * channels + chan * half + at, times, stride=2 * channels), :] = mine
                spread[pl.ds(ri * channels + (1 - chan) * half + at, times, stride=2 * channels), :] = theirs

    barrier = pltpu.get_barrier_semaphore()
    for other in others:
        pl.semaphore_signal(barrier, inc=1, device_id=other, device_id_type=MESH)

    @pl.loop(0, CHUNKS)
    def _(k):
        fetch_volt(k).start()

    @pl.loop(0, CHUNKS)
    def _(k):
        fetch_weight(k).start()

    pl.semaphore_wait(barrier, len(others))

    def stage(tick, lag, work):
        k = tick - lag

        @pl.when(jnp.logical_and(k >= 0, k < CHUNKS))
        def _():
            work(k)

    def first(k):
        fetch_volt(k).wait()
        z_hop(k, 0, 0)
        z_hop(k, 1, 0)

    def onward(distance):
        def work(k):
            z_hop(k, 0, distance)
            z_hop(k, 1, distance)

        return work

    def products(k):
        multiply(k)
        send_early(k)

    @pl.loop(0, CHUNKS + 9)
    def _(tick):
        stage(tick, 0, first)
        for distance in range(1, 5):
            stage(tick, distance, onward(distance))
        stage(tick, 5, products)
        stage(tick, 6, send_late)
        stage(tick, 7, send_cross)
        stage(tick, 8, gather)

    size = channels
    for t in range(0, times, 2):
        left = spread[t * 2 * size:(t + 1) * 2 * size, :].astype(jnp.bfloat16)
        right = spread[(t + 1) * 2 * size:(t + 2) * 2 * size, :].astype(jnp.bfloat16)
        fine = jnp.dot(table_ref[...], jnp.concatenate([left, right], axis=1), preferred_element_type=jnp.float32)
        real = fine[0:size] + fine[2 * size:3 * size]
        imag = fine[size:2 * size] + fine[3 * size:4 * size]
        power = real * real + imag * imag
        beams = power_ref.shape[1]
        power_ref[pl.ds(t, size, stride=times), :] = power[:, :beams]
        power_ref[pl.ds(t + 1, size, stride=times), :] = power[:, beams:]

    for side in (0, 1):
        await_bytes(volt.at[0, :, pl.ds(0, 7)], z_send.at[side])
        await_bytes(volt.at[0, :, pl.ds(0, 6)], y_send.at[side])
    await_bytes(volt.at[0], mate_send)
    await_bytes(volt.at[0, :, pl.ds(0, 3)], x_send)


def shards(voltages, weights):
    _, own, times, width = voltages.shape
    beams = weights.shape[3]
    owners = 2 * Z
    channels = 2 * own
    per = own // CHUNKS
    table = jnp.asarray(synthesis_table(channels))
    bf16, f32 = jnp.bfloat16, jnp.float32
    dma = pltpu.SemaphoreType.DMA
    power = pl.pallas_call(
        kernel,
        out_shape=jax.ShapeDtypeStruct((channels * times, beams), f32),
        in_specs=[
            pl.BlockSpec(memory_space=pl.ANY),
            pl.BlockSpec(memory_space=pl.ANY),
            pl.BlockSpec(memory_space=pltpu.VMEM),
        ],
        out_specs=pl.BlockSpec(memory_space=pltpu.VMEM),
        scratch_shapes=[
            pltpu.VMEM((2, own, owners, times, width), bf16),
            pltpu.VMEM((2, own, width, beams), bf16),
            pltpu.VMEM((CHUNKS, 2, per, 2, Y, 2, times, beams), bf16),
            pltpu.VMEM((CHUNKS, 2, per, 2, 2, times, beams), bf16),
            pltpu.VMEM((CHUNKS, 2, 2, per, 2, 2, times, beams), bf16),
            pltpu.VMEM((CHUNKS, 3, 2, per, times, beams), bf16),
            pltpu.VMEM((times * 2 * channels, beams), f32),
            dma((CHUNKS,)),
            dma((CHUNKS,)),
            dma((2, 4, CHUNKS)),
            dma((CHUNKS,)),
            dma((2, CHUNKS)),
            dma((2, CHUNKS)),
            dma((CHUNKS,)),
            dma((2,)),
            dma,
            dma((2,)),
            dma,
        ],
        compiler_params=pltpu.CompilerParams(
            collective_id=0, has_side_effects=True, vmem_limit_bytes=60 * 2**20
        ),
        name="beamform",
    )(voltages, weights, table)
    return power.reshape(channels, times, beams)


def solution(mesh):
    placed = (P(None, "chan", "beam", "elem"), P(None, "chan", "elem", "beam"))
    return jax.shard_map(
        shards,
        mesh=mesh,
        in_specs=placed,
        out_specs=P(None, ("chan", "elem"), "beam"),
        check_vma=False,
    )
```

```python
import jax
import jax.numpy as jnp
import numpy as np
from jax import lax
from jax.experimental import pallas as pl
from jax.experimental.pallas import tpu as pltpu
from jax.sharding import PartitionSpec as P

MESH = pl.DeviceIdType.MESH

X, Y, Z = 4, 4, 8
CHUNKS = ((20, 3), (2, 2))
ORDER = (('products', 7), (3, 5), (4, 6), ('mate', 6), (0, 0), ('late', 8), (1, 2), ('gather', 14), ('cross', 10), (2, 3))


def synthesis_table(channels):
    index = np.arange(channels)
    angle = (index[:, None] * index[None, :] % channels) * (2.0 * np.pi / channels)
    cosine, sine = np.cos(angle) / np.sqrt(channels), np.sin(angle) / np.sqrt(channels)
    table = np.block([[cosine, -sine], [sine, cosine]]).astype(np.float32)
    high = table.astype(jnp.bfloat16)
    low = (table - high.astype(np.float32)).astype(jnp.bfloat16)
    return np.concatenate([high, low], axis=0)


def kernel(
    volt_hbm, weight_hbm, table_hbm, power_ref,
    volt, weight, part, early, late, cross, spread, table,
    volt_in, weight_in, table_in, z_recv, mate_recv, early_recv, late_recv, cross_recv,
    z_send, mate_send, y_send, x_send,
):
    chan, elem, beam = lax.axis_index("chan"), lax.axis_index("elem"), lax.axis_index("beam")
    z, core = beam // 2, beam % 2
    y, x_hi = elem // 2, elem % 2
    x = x_hi * 2 + chan
    times = volt.shape[4]
    channels = 2 * volt.shape[0]
    chunks = sum(count for count, _ in CHUNKS)

    def at_z(step):
        return (chan, elem, lax.rem(z + step + Z, Z) * 2 + core)

    def at_y(step):
        return (chan, lax.rem(y + step + Y, Y) * 2 + x_hi, beam)

    def at_x(step):
        to = lax.rem(x + step, X)
        return (to % 2, y * 2 + to // 2, beam)

    mate = (chan, elem, z * 2 + (1 - core))
    others = [mate, at_z(1), at_z(-1), at_y(1), at_y(-1), at_x(1), at_x(2), at_x(3)]

    def fetch_volt(k, at):
        for ri in (0, 1):
            pltpu.make_async_copy(volt_hbm.at[ri, at], volt.at[at, core, z, ri], volt_in.at[k]).start()

    def fetch_weight(k, at):
        return pltpu.make_async_copy(weight_hbm.at[:, at], weight.at[:, at], weight_in.at[k])

    fetch_table = pltpu.make_async_copy(table_hbm, table, table_in)

    def send(src, dst, send_sem, recv_sem, to):
        pltpu.make_async_remote_copy(
            src_ref=src, dst_ref=dst, send_sem=send_sem, recv_sem=recv_sem, device_id=to, device_id_type=MESH
        ).start()

    def await_bytes(like, sem):
        pltpu.make_async_copy(like, like, sem).wait()

    def piece(at, owner, half=None):
        return volt.at[at, core, owner] if half is None else volt.at[at, core, owner, half]

    def z_hop(k, at, side, distance):
        owner = lax.rem(z + (distance if side else -distance) + Z, Z)
        if distance:
            await_bytes(piece(at, owner, side if distance == 4 else None), z_recv.at[side, distance - 1, k])
        if distance < 4:
            moved = piece(at, owner, side if distance == 3 else None)
            send(moved, moved, z_send.at[side], z_recv.at[side, distance, k], at_z(-1 if side else 1))

    def to_y(step):
        return lax.rem(y + step + Y, Y)

    def multiply(k, at):
        fetch_weight(k, at).wait()
        await_bytes(volt.at[at, 0], mate_recv.at[k])

        @pl.loop(0, at.size)
        def _(step):
            c = at.start + step
            width, beams = volt.shape[5], weight.shape[3]
            both = jnp.concatenate([weight[0, c], weight[1, c]], axis=1)

            def times_both(ri):
                rows = jnp.stack([volt[c, 0, :, ri], volt[c, 1, :, ri]], axis=1)
                return jnp.dot(rows.reshape(2 * Z * times, width), both, preferred_element_type=jnp.float32)

            with_real, with_imag = times_both(0), times_both(1)
            real = (with_real[:, :beams] - with_imag[:, beams:]).astype(jnp.bfloat16)
            imag = (with_real[:, beams:] + with_imag[:, :beams]).astype(jnp.bfloat16)
            for ri, value in enumerate((real, imag)):
                value = value.reshape(2, Y, 2, times, beams)
                for lo in (0, 1):
                    part[c, :, ri, lo] = value[lo]

    def send_mate(k, at):
        send(volt.at[at, core], volt.at[at, core], mate_send, mate_recv.at[k], mate)

    def send_early(k, at):
        for side in (0, 1):
            send(
                part.at[at, to_y(2), side], early.at[at, side], y_send.at[side], early_recv.at[side, k],
                at_y(-1 if side else 1),
            )

    def send_late(k, at):
        for side in (0, 1):
            near = to_y(-1 if side else 1)
            await_bytes(early.at[at, side], early_recv.at[side, k])
            total = part[at, near, side].astype(jnp.float32) + early[at, side].astype(jnp.float32)
            part[at, near, side] = total.astype(jnp.bfloat16)
            send(
                part.at[at, near], late.at[at, side], y_send.at[side], late_recv.at[side, k], at_y(-1 if side else 1)
            )

    def send_cross(k, at):
        for side in (0, 1):
            await_bytes(late.at[at, side], late_recv.at[side, k])
        total = part[at, y].astype(jnp.float32) + late[at, 0].astype(jnp.float32) + late[at, 1].astype(jnp.float32)
        part[at, y] = total.astype(jnp.bfloat16)
        for step in (2, 1, 3):
            to = lax.rem(x + step, X)
            send(
                part.at[at, y, :, to % 2, to // 2], cross.at[at, step - 1], x_send, cross_recv.at[k], at_x(step)
            )

    def gather(k, at):
        await_bytes(cross.at[at], cross_recv.at[k])
        half = channels // 2
        for ri in (0, 1):
            for step in range(at.size):
                c = at.start + step
                row = ri * channels + c
                mine = part[c, y, ri, chan, x_hi].astype(jnp.float32) + cross[c, 1, ri].astype(jnp.float32)
                theirs = cross[c, 0, ri].astype(jnp.float32) + cross[c, 2, ri].astype(jnp.float32)
                spread[pl.ds(chan * half + row, times, stride=2 * channels), :] = mine
                spread[pl.ds((1 - chan) * half + row, times, stride=2 * channels), :] = theirs

    def in_chunk(k, work):
        chunk, channel = 0, 0
        for count, size in CHUNKS:

            @pl.when(jnp.logical_and(k >= chunk, k < chunk + count))
            def _():
                work(k, pl.ds(channel + (k - chunk) * size, size))

            chunk, channel = chunk + count, channel + count * size

    barrier = pltpu.get_barrier_semaphore()
    for other in others:
        pl.semaphore_signal(barrier, inc=1, device_id=other, device_id_type=MESH)

    @pl.loop(0, chunks)
    def _(k):
        in_chunk(k, fetch_volt)

    @pl.loop(0, chunks)
    def _(k):
        in_chunk(k, lambda k, at: fetch_weight(k, at).start())

    fetch_table.start()
    pl.semaphore_wait(barrier, len(others))

    def z_stage(distance):
        def work(k, at):
            if distance == 0:
                await_bytes(piece(at, z), volt_in.at[k])
            for side in (0, 1):
                z_hop(k, at, side, distance)

        return work

    def products(k, at):
        multiply(k, at)
        send_early(k, at)

    stages = {"mate": send_mate, "products": products, "late": send_late, "cross": send_cross, "gather": gather}
    stages.update((distance, z_stage(distance)) for distance in range(5))

    @pl.loop(0, chunks + max(lag for _, lag in ORDER))
    def _(tick):
        for stage, lag in ORDER:
            in_chunk(tick - lag, stages[stage])

    fetch_table.wait()

    size = channels
    for t in range(0, times, 2):
        left = spread[t * 2 * size:(t + 1) * 2 * size, :].astype(jnp.bfloat16)
        right = spread[(t + 1) * 2 * size:(t + 2) * 2 * size, :].astype(jnp.bfloat16)
        fine = jnp.dot(table[...], jnp.concatenate([left, right], axis=1), preferred_element_type=jnp.float32)
        real = fine[0:size] + fine[2 * size:3 * size]
        imag = fine[size:2 * size] + fine[3 * size:4 * size]
        power = real * real + imag * imag
        beams = power_ref.shape[1]
        power_ref[pl.ds(t, size, stride=times), :] = power[:, :beams]
        power_ref[pl.ds(t + 1, size, stride=times), :] = power[:, beams:]

    for side in (0, 1):
        await_bytes(volt.at[:, 0, 0:7, 0], z_send.at[side])
        await_bytes(volt.at[:, 0, 0:3], y_send.at[side])
    await_bytes(volt.at[:, 0], mate_send)
    await_bytes(cross, x_send)


def shards(voltages, weights):
    _, own, times, width = voltages.shape
    beams = weights.shape[3]
    channels = 2 * own
    chunks = sum(count for count, _ in CHUNKS)
    table = jnp.asarray(synthesis_table(channels))
    bf16, f32 = jnp.bfloat16, jnp.float32
    dma = pltpu.SemaphoreType.DMA
    power = pl.pallas_call(
        kernel,
        out_shape=jax.ShapeDtypeStruct((channels * times, beams), f32),
        in_specs=[pl.BlockSpec(memory_space=pltpu.HBM)] * 3,
        out_specs=pl.BlockSpec(memory_space=pltpu.VMEM),
        scratch_shapes=[
            pltpu.VMEM((own, 2, Z, 2, times, width), bf16),
            pltpu.VMEM((2, own, width, beams), bf16),
            pltpu.VMEM((own, Y, 2, 2, 2, times, beams), bf16),
            pltpu.VMEM((own, 2, 2, 2, times, beams), bf16),
            pltpu.VMEM((own, 2, 2, 2, 2, times, beams), bf16),
            pltpu.VMEM((own, 3, 2, times, beams), bf16),
            pltpu.VMEM((times * 2 * channels, beams), f32),
            pltpu.VMEM(table.shape, bf16),
            dma((chunks,)),
            dma((chunks,)),
            dma,
            dma((2, 4, chunks)),
            dma((chunks,)),
            dma((2, chunks)),
            dma((2, chunks)),
            dma((chunks,)),
            dma((2,)),
            dma,
            dma((2,)),
            dma,
        ],
        compiler_params=pltpu.CompilerParams(
            collective_id=0, has_side_effects=True, vmem_limit_bytes=46 * 2**20
        ),
        name="beamform",
    )(voltages, weights, table)
    return power.reshape(channels, times, beams)


def solution(mesh):
    placed = (P(None, "chan", "beam", "elem"), P(None, "chan", "elem", "beam"))
    return jax.shard_map(
        shards,
        mesh=mesh,
        in_specs=placed,
        out_specs=P(None, ("chan", "elem"), "beam"),
        check_vma=False,
    )
```

```python
import jax
import jax.numpy as jnp
import numpy as np
from jax import lax
from jax.experimental import pallas as pl
from jax.experimental.pallas import tpu as pltpu
from jax.sharding import PartitionSpec as P

MESH = pl.DeviceIdType.MESH

X, Y, Z = 4, 4, 8
CHUNKS = ((18, 3), (5, 2))
ORDER = ((3, 5), (4, 6), ('mate', 6), ('gather', 14), ('late', 8), (0, 0), (1, 2), ('cross', 10), (2, 3), ('products', 6))


def synthesis_table(channels):
    index = np.arange(channels)
    angle = (index[:, None] * index[None, :] % channels) * (2.0 * np.pi / channels)
    cosine, sine = np.cos(angle) / np.sqrt(channels), np.sin(angle) / np.sqrt(channels)
    table = np.block([[cosine, -sine], [sine, cosine]]).astype(np.float32)
    high = table.astype(jnp.bfloat16)
    low = (table - high.astype(np.float32)).astype(jnp.bfloat16)
    return np.concatenate([high, low], axis=0)


def kernel(
    volt_hbm, weight_hbm, table_hbm, power_ref,
    volt, weight, part, early, late, cross, spread, table,
    volt_in, weight_in, table_in, z_recv, mate_recv, early_recv, late_recv, cross_recv,
    z_send, mate_send, y_send, x_send,
):
    chan, elem, beam = lax.axis_index("chan"), lax.axis_index("elem"), lax.axis_index("beam")
    z, core = beam // 2, beam % 2
    y, x_hi = elem // 2, elem % 2
    x = x_hi * 2 + chan
    times = volt.shape[4]
    channels = 2 * volt.shape[0]
    chunks = sum(count for count, _ in CHUNKS)

    def at_z(step):
        return (chan, elem, lax.rem(z + step + Z, Z) * 2 + core)

    def at_y(step):
        return (chan, lax.rem(y + step + Y, Y) * 2 + x_hi, beam)

    def at_x(step):
        to = lax.rem(x + step, X)
        return (to % 2, y * 2 + to // 2, beam)

    mate = (chan, elem, z * 2 + (1 - core))
    others = [mate, at_z(1), at_z(-1), at_y(1), at_y(-1), at_x(1), at_x(2), at_x(3)]

    def fetch_volt(k, at):
        for ri in (0, 1):
            pltpu.make_async_copy(volt_hbm.at[ri, at], volt.at[at, core, z, ri], volt_in.at[k]).start()

    def fetch_weight(k, at):
        return pltpu.make_async_copy(weight_hbm.at[:, at], weight.at[:, at], weight_in.at[k])

    fetch_table = pltpu.make_async_copy(table_hbm, table, table_in)

    def send(src, dst, send_sem, recv_sem, to):
        pltpu.make_async_remote_copy(
            src_ref=src, dst_ref=dst, send_sem=send_sem, recv_sem=recv_sem, device_id=to, device_id_type=MESH
        ).start()

    def await_bytes(like, sem):
        pltpu.make_async_copy(like, like, sem).wait()

    def piece(at, owner, half=None):
        return volt.at[at, core, owner] if half is None else volt.at[at, core, owner, half]

    def z_hop(k, at, side, distance):
        owner = lax.rem(z + (distance if side else -distance) + Z, Z)
        if distance:
            await_bytes(piece(at, owner, side if distance == 4 else None), z_recv.at[side, distance - 1, k])
        if distance < 4:
            moved = piece(at, owner, side if distance == 3 else None)
            send(moved, moved, z_send.at[side], z_recv.at[side, distance, k], at_z(-1 if side else 1))

    def to_y(step):
        return lax.rem(y + step + Y, Y)

    def multiply(k, at):
        fetch_weight(k, at).wait()
        await_bytes(volt.at[at, 0], mate_recv.at[k])

        @pl.loop(0, at.size)
        def _(step):
            c = at.start + step
            width, beams = volt.shape[5], weight.shape[3]
            both = jnp.concatenate([weight[0, c], weight[1, c]], axis=1)

            def times_both(ri):
                rows = jnp.stack([volt[c, 0, :, ri], volt[c, 1, :, ri]], axis=1)
                return jnp.dot(rows.reshape(2 * Z * times, width), both, preferred_element_type=jnp.float32)

            with_real, with_imag = times_both(0), times_both(1)
            real = (with_real[:, :beams] - with_imag[:, beams:]).astype(jnp.bfloat16)
            imag = (with_real[:, beams:] + with_imag[:, :beams]).astype(jnp.bfloat16)
            for ri, value in enumerate((real, imag)):
                value = value.reshape(2, Y, 2, times, beams)
                for lo in (0, 1):
                    part[c, :, ri, lo] = value[lo]

    def send_mate(k, at):
        send(volt.at[at, core], volt.at[at, core], mate_send, mate_recv.at[k], mate)

    def send_early(k, at):
        for side in (0, 1):
            send(
                part.at[at, to_y(2), side], early.at[at, side], y_send.at[side], early_recv.at[side, k],
                at_y(-1 if side else 1),
            )

    def send_late(k, at):
        for side in (0, 1):
            near = to_y(-1 if side else 1)
            await_bytes(early.at[at, side], early_recv.at[side, k])
            total = part[at, near, side].astype(jnp.float32) + early[at, side].astype(jnp.float32)
            part[at, near, side] = total.astype(jnp.bfloat16)
            send(
                part.at[at, near], late.at[at, side], y_send.at[side], late_recv.at[side, k], at_y(-1 if side else 1)
            )

    def send_cross(k, at):
        for side in (0, 1):
            await_bytes(late.at[at, side], late_recv.at[side, k])
        total = part[at, y].astype(jnp.float32) + late[at, 0].astype(jnp.float32) + late[at, 1].astype(jnp.float32)
        part[at, y] = total.astype(jnp.bfloat16)
        for step in (2, 1, 3):
            to = lax.rem(x + step, X)
            send(
                part.at[at, y, :, to % 2, to // 2], cross.at[at, step - 1], x_send, cross_recv.at[k], at_x(step)
            )

    def gather(k, at):
        await_bytes(cross.at[at], cross_recv.at[k])
        half = channels // 2
        for ri in (0, 1):
            for step in range(at.size):
                c = at.start + step
                row = ri * channels + c
                mine = part[c, y, ri, chan, x_hi].astype(jnp.float32) + cross[c, 1, ri].astype(jnp.float32)
                theirs = cross[c, 0, ri].astype(jnp.float32) + cross[c, 2, ri].astype(jnp.float32)
                spread[pl.ds(chan * half + row, times, stride=2 * channels), :] = mine
                spread[pl.ds((1 - chan) * half + row, times, stride=2 * channels), :] = theirs

    def in_chunk(k, work):
        chunk, channel = 0, 0
        for count, size in CHUNKS:

            @pl.when(jnp.logical_and(k >= chunk, k < chunk + count))
            def _():
                work(k, pl.ds(channel + (k - chunk) * size, size))

            chunk, channel = chunk + count, channel + count * size

    barrier = pltpu.get_barrier_semaphore()
    for other in others:
        pl.semaphore_signal(barrier, inc=1, device_id=other, device_id_type=MESH)

    @pl.loop(0, chunks)
    def _(k):
        in_chunk(k, fetch_volt)

    @pl.loop(0, chunks)
    def _(k):
        in_chunk(k, lambda k, at: fetch_weight(k, at).start())

    fetch_table.start()
    pl.semaphore_wait(barrier, len(others))

    def z_stage(distance):
        def work(k, at):
            if distance == 0:
                await_bytes(piece(at, z), volt_in.at[k])
            for side in (0, 1):
                z_hop(k, at, side, distance)

        return work

    def products(k, at):
        multiply(k, at)
        send_early(k, at)

    stages = {"mate": send_mate, "products": products, "late": send_late, "cross": send_cross, "gather": gather}
    stages.update((distance, z_stage(distance)) for distance in range(5))

    @pl.loop(0, chunks + max(lag for _, lag in ORDER))
    def _(tick):
        for stage, lag in ORDER:
            in_chunk(tick - lag, stages[stage])

    fetch_table.wait()

    size = channels
    for t in range(0, times, 2):
        left = spread[t * 2 * size:(t + 1) * 2 * size, :].astype(jnp.bfloat16)
        right = spread[(t + 1) * 2 * size:(t + 2) * 2 * size, :].astype(jnp.bfloat16)
        fine = jnp.dot(table[...], jnp.concatenate([left, right], axis=1), preferred_element_type=jnp.float32)
        real = fine[0:size] + fine[2 * size:3 * size]
        imag = fine[size:2 * size] + fine[3 * size:4 * size]
        power = real * real + imag * imag
        beams = power_ref.shape[1]
        power_ref[pl.ds(t, size, stride=times), :] = power[:, :beams]
        power_ref[pl.ds(t + 1, size, stride=times), :] = power[:, beams:]

    for side in (0, 1):
        await_bytes(volt.at[:, 0, 0:7, 0], z_send.at[side])
        await_bytes(volt.at[:, 0, 0:3], y_send.at[side])
    await_bytes(volt.at[:, 0], mate_send)
    await_bytes(cross, x_send)


def shards(voltages, weights):
    _, own, times, width = voltages.shape
    beams = weights.shape[3]
    channels = 2 * own
    chunks = sum(count for count, _ in CHUNKS)
    table = jnp.asarray(synthesis_table(channels))
    bf16, f32 = jnp.bfloat16, jnp.float32
    dma = pltpu.SemaphoreType.DMA
    power = pl.pallas_call(
        kernel,
        out_shape=jax.ShapeDtypeStruct((channels * times, beams), f32),
        in_specs=[pl.BlockSpec(memory_space=pltpu.HBM)] * 3,
        out_specs=pl.BlockSpec(memory_space=pltpu.VMEM),
        scratch_shapes=[
            pltpu.VMEM((own, 2, Z, 2, times, width), bf16),
            pltpu.VMEM((2, own, width, beams), bf16),
            pltpu.VMEM((own, Y, 2, 2, 2, times, beams), bf16),
            pltpu.VMEM((own, 2, 2, 2, times, beams), bf16),
            pltpu.VMEM((own, 2, 2, 2, 2, times, beams), bf16),
            pltpu.VMEM((own, 3, 2, times, beams), bf16),
            pltpu.VMEM((times * 2 * channels, beams), f32),
            pltpu.VMEM(table.shape, bf16),
            dma((chunks,)),
            dma((chunks,)),
            dma,
            dma((2, 4, chunks)),
            dma((chunks,)),
            dma((2, chunks)),
            dma((2, chunks)),
            dma((chunks,)),
            dma((2,)),
            dma,
            dma((2,)),
            dma,
        ],
        compiler_params=pltpu.CompilerParams(
            collective_id=0, has_side_effects=True, vmem_limit_bytes=46 * 2**20
        ),
        name="beamform",
    )(*(pltpu.with_memory_space_constraint(v, pltpu.HBM) for v in (voltages, weights, table)))
    return power.reshape(channels, times, beams)


def solution(mesh):
    placed = (P(None, "chan", "beam", "elem"), P(None, "chan", "elem", "beam"))
    return jax.shard_map(
        shards,
        mesh=mesh,
        in_specs=placed,
        out_specs=P(None, ("chan", "elem"), "beam"),
        check_vma=False,
    )
```

```python
import jax
import jax.numpy as jnp
import numpy as np
from jax import lax
from jax.experimental import pallas as pl
from jax.experimental.pallas import tpu as pltpu
from jax.sharding import PartitionSpec as P

MESH = pl.DeviceIdType.MESH

X, Y, Z = 4, 4, 8
CHUNKS = ((18, 3), (5, 2))
ORDER = ((3, 5), (4, 6), ('mate', 6), ('gather', 14), ('late', 8), (0, 0), (1, 2), ('cross', 10), (2, 3), ('products', 6))


def synthesis_table(channels):
    index = np.arange(channels)
    angle = (index[:, None] * index[None, :] % channels) * (2.0 * np.pi / channels)
    cosine, sine = np.cos(angle) / np.sqrt(channels), np.sin(angle) / np.sqrt(channels)
    table = np.block([[cosine, -sine], [sine, cosine]]).astype(np.float32)
    high = table.astype(jnp.bfloat16)
    low = (table - high.astype(np.float32)).astype(jnp.bfloat16)
    return np.concatenate([high, low], axis=0)


def kernel(
    volt_hbm, weight_hbm, table_hbm, power_ref,
    volt, weight, part, early, late, cross, spread, table,
    volt_in, weight_in, table_in, z_recv, mate_recv, early_recv, late_recv, cross_recv,
    z_send, mate_send, y_send, x_send,
):
    chan, elem, beam = lax.axis_index("chan"), lax.axis_index("elem"), lax.axis_index("beam")
    z, core = beam // 2, beam % 2
    y, x_hi = elem // 2, elem % 2
    x = x_hi * 2 + chan
    times = volt.shape[4]
    channels = 2 * volt.shape[0]
    chunks = sum(count for count, _ in CHUNKS)

    def at_z(step):
        return (chan, elem, lax.rem(z + step + Z, Z) * 2 + core)

    def at_y(step):
        return (chan, lax.rem(y + step + Y, Y) * 2 + x_hi, beam)

    def at_x(step):
        to = lax.rem(x + step, X)
        return (to % 2, y * 2 + to // 2, beam)

    mate = (chan, elem, z * 2 + (1 - core))
    others = [mate, at_z(1), at_z(-1), at_y(1), at_y(-1), at_x(1), at_x(2), at_x(3)]

    def fetch_volt(k, at):
        for ri in (0, 1):
            pltpu.make_async_copy(volt_hbm.at[ri, at], volt.at[at, core, z, ri], volt_in.at[k]).start()

    def fetch_weight(k, at):
        return pltpu.make_async_copy(weight_hbm.at[:, at], weight.at[:, at], weight_in.at[k])

    fetch_table = pltpu.make_async_copy(table_hbm, table, table_in)

    def send(src, dst, send_sem, recv_sem, to):
        pltpu.make_async_remote_copy(
            src_ref=src, dst_ref=dst, send_sem=send_sem, recv_sem=recv_sem, device_id=to, device_id_type=MESH
        ).start()

    def await_bytes(like, sem):
        pltpu.make_async_copy(like, like, sem).wait()

    def piece(at, owner, half=None):
        return volt.at[at, core, owner] if half is None else volt.at[at, core, owner, half]

    def z_hop(k, at, side, distance):
        owner = lax.rem(z + (distance if side else -distance) + Z, Z)
        if distance:
            await_bytes(piece(at, owner, side if distance == 4 else None), z_recv.at[side, distance - 1, k])
        if distance < 4:
            moved = piece(at, owner, side if distance == 3 else None)
            send(moved, moved, z_send.at[side], z_recv.at[side, distance, k], at_z(-1 if side else 1))

    def to_y(step):
        return lax.rem(y + step + Y, Y)

    def multiply(k, at):
        fetch_weight(k, at).wait()
        await_bytes(volt.at[at, 0], mate_recv.at[k])

        @pl.loop(0, at.size)
        def _(step):
            c = at.start + step
            width, beams = volt.shape[5], weight.shape[3]
            both = jnp.concatenate([weight[0, c], weight[1, c]], axis=1)

            def times_both(ri):
                rows = jnp.stack([volt[c, 0, :, ri], volt[c, 1, :, ri]], axis=1)
                return jnp.dot(rows.reshape(2 * Z * times, width), both, preferred_element_type=jnp.float32)

            with_real, with_imag = times_both(0), times_both(1)
            real = (with_real[:, :beams] - with_imag[:, beams:]).astype(jnp.bfloat16)
            imag = (with_real[:, beams:] + with_imag[:, :beams]).astype(jnp.bfloat16)
            for ri, value in enumerate((real, imag)):
                value = value.reshape(2, Y, 2, times, beams)
                for lo in (0, 1):
                    part[c, :, ri, lo] = value[lo]

    def send_mate(k, at):
        send(volt.at[at, core], volt.at[at, core], mate_send, mate_recv.at[k], mate)

    def send_early(k, at):
        for side in (0, 1):
            send(
                part.at[at, to_y(2), side], early.at[at, side], y_send.at[side], early_recv.at[side, k],
                at_y(-1 if side else 1),
            )
        if at.size < CHUNKS[0][1]:
            for side in (0, 1):
                near, half = to_y(-1 if side else 1), 1 - side
                send(
                    part.at[at, near, half], late.at[at, side, half], y_send.at[side], late_recv.at[side, k],
                    at_y(-1 if side else 1),
                )

    def send_late(k, at):
        for side in (0, 1):
            near = to_y(-1 if side else 1)
            await_bytes(early.at[at, side], early_recv.at[side, k])
            total = part[at, near, side].astype(jnp.float32) + early[at, side].astype(jnp.float32)
            part[at, near, side] = total.astype(jnp.bfloat16)
            whole = at.size == CHUNKS[0][1]
            send(
                part.at[at, near] if whole else part.at[at, near, side],
                late.at[at, side] if whole else late.at[at, side, side],
                y_send.at[side], late_recv.at[side, k], at_y(-1 if side else 1),
            )

    def send_cross(k, at):
        for side in (0, 1):
            await_bytes(late.at[at, side], late_recv.at[side, k])
        total = part[at, y].astype(jnp.float32) + late[at, 0].astype(jnp.float32) + late[at, 1].astype(jnp.float32)
        part[at, y] = total.astype(jnp.bfloat16)
        for step in (2, 1, 3):
            to = lax.rem(x + step, X)
            send(
                part.at[at, y, :, to % 2, to // 2], cross.at[at, step - 1], x_send, cross_recv.at[k], at_x(step)
            )

    def gather(k, at):
        await_bytes(cross.at[at], cross_recv.at[k])
        half = channels // 2
        for ri in (0, 1):
            for step in range(at.size):
                c = at.start + step
                row = ri * channels + c
                mine = part[c, y, ri, chan, x_hi].astype(jnp.float32) + cross[c, 1, ri].astype(jnp.float32)
                theirs = cross[c, 0, ri].astype(jnp.float32) + cross[c, 2, ri].astype(jnp.float32)
                spread[pl.ds(chan * half + row, times, stride=2 * channels), :] = mine
                spread[pl.ds((1 - chan) * half + row, times, stride=2 * channels), :] = theirs

    def in_chunk(k, work):
        chunk, channel = 0, 0
        for count, size in CHUNKS:

            @pl.when(jnp.logical_and(k >= chunk, k < chunk + count))
            def _():
                work(k, pl.ds(channel + (k - chunk) * size, size))

            chunk, channel = chunk + count, channel + count * size

    barrier = pltpu.get_barrier_semaphore()
    for other in others:
        pl.semaphore_signal(barrier, inc=1, device_id=other, device_id_type=MESH)

    @pl.loop(0, chunks)
    def _(k):
        in_chunk(k, fetch_volt)

    @pl.loop(0, chunks)
    def _(k):
        in_chunk(k, lambda k, at: fetch_weight(k, at).start())

    fetch_table.start()
    pl.semaphore_wait(barrier, len(others))

    def z_stage(distance):
        def work(k, at):
            if distance == 0:
                await_bytes(piece(at, z), volt_in.at[k])
            for side in (0, 1):
                z_hop(k, at, side, distance)

        return work

    def products(k, at):
        multiply(k, at)
        send_early(k, at)

    stages = {"mate": send_mate, "products": products, "late": send_late, "cross": send_cross, "gather": gather}
    stages.update((distance, z_stage(distance)) for distance in range(5))

    @pl.loop(0, chunks + max(lag for _, lag in ORDER))
    def _(tick):
        for stage, lag in ORDER:
            in_chunk(tick - lag, stages[stage])

    fetch_table.wait()

    size = channels
    for t in range(0, times, 2):
        left = spread[t * 2 * size:(t + 1) * 2 * size, :].astype(jnp.bfloat16)
        right = spread[(t + 1) * 2 * size:(t + 2) * 2 * size, :].astype(jnp.bfloat16)
        fine = jnp.dot(table[...], jnp.concatenate([left, right], axis=1), preferred_element_type=jnp.float32)
        real = fine[0:size] + fine[2 * size:3 * size]
        imag = fine[size:2 * size] + fine[3 * size:4 * size]
        power = real * real + imag * imag
        beams = power_ref.shape[1]
        power_ref[pl.ds(t, size, stride=times), :] = power[:, :beams]
        power_ref[pl.ds(t + 1, size, stride=times), :] = power[:, beams:]

    for side in (0, 1):
        await_bytes(volt.at[:, 0, 0:7, 0], z_send.at[side])
        await_bytes(volt.at[:, 0, 0:3], y_send.at[side])
    await_bytes(volt.at[:, 0], mate_send)
    await_bytes(cross, x_send)


def shards(voltages, weights):
    _, own, times, width = voltages.shape
    beams = weights.shape[3]
    channels = 2 * own
    chunks = sum(count for count, _ in CHUNKS)
    table = jnp.asarray(synthesis_table(channels))
    bf16, f32 = jnp.bfloat16, jnp.float32
    dma = pltpu.SemaphoreType.DMA
    power = pl.pallas_call(
        kernel,
        out_shape=jax.ShapeDtypeStruct((channels * times, beams), f32),
        in_specs=[pl.BlockSpec(memory_space=pltpu.HBM)] * 3,
        out_specs=pl.BlockSpec(memory_space=pltpu.VMEM),
        scratch_shapes=[
            pltpu.VMEM((own, 2, Z, 2, times, width), bf16),
            pltpu.VMEM((2, own, width, beams), bf16),
            pltpu.VMEM((own, Y, 2, 2, 2, times, beams), bf16),
            pltpu.VMEM((own, 2, 2, 2, times, beams), bf16),
            pltpu.VMEM((own, 2, 2, 2, 2, times, beams), bf16),
            pltpu.VMEM((own, 3, 2, times, beams), bf16),
            pltpu.VMEM((times * 2 * channels, beams), f32),
            pltpu.VMEM(table.shape, bf16),
            dma((chunks,)),
            dma((chunks,)),
            dma,
            dma((2, 4, chunks)),
            dma((chunks,)),
            dma((2, chunks)),
            dma((2, chunks)),
            dma((chunks,)),
            dma((2,)),
            dma,
            dma((2,)),
            dma,
        ],
        compiler_params=pltpu.CompilerParams(
            collective_id=0, has_side_effects=True, vmem_limit_bytes=46 * 2**20
        ),
        name="beamform",
    )(*(pltpu.with_memory_space_constraint(v, pltpu.HBM) for v in (voltages, weights, table)))
    return power.reshape(channels, times, beams)


def solution(mesh):
    placed = (P(None, "chan", "beam", "elem"), P(None, "chan", "elem", "beam"))
    return jax.shard_map(
        shards,
        mesh=mesh,
        in_specs=placed,
        out_specs=P(None, ("chan", "elem"), "beam"),
        check_vma=False,
    )
```
